128 devices in a mesh: pop: 16 (over y, x_lo, core), batch: 8 (over z, x_hi).
Axes of the slice: x: 4 (x_hi: 2, x_lo: 2; x = x_hi * 2 + x_lo), y: 4, z: 4, core: 2. Of those that a mesh axis runs over, the one named last changes fastest.
Arguments:
- observations: bfloat16 [2048, 512], P('batch'), may hold values from -6 to 6
- rewards: bfloat16 [2048, 128], P('batch'), may hold values from -6 to 6
- new_first: bfloat16 [32, 512, 1024], P('pop'), may hold values from -0.25 to 0.25
- new_second: bfloat16 [32, 1024, 512], P('pop'), may hold values from -0.1875 to 0.1875
- pop_first: bfloat16 [16, 512, 1024], P('pop'), may hold values from -0.25 to 0.25
- pop_second: bfloat16 [16, 1024, 128], P('pop'), may hold values from -0.1875 to 0.1875
- faces: int32 [32, 16], P('pop'), may hold values 0 or 1
Outputs:
- payoff: float32 [32, 16], P('pop')
The draws below stay inside these ranges and needn't reach their ends.
All inputs are finite; a program needn't handle non-finite values. No bound on the sum of `faces` on one device may be relied on, other than what follows from the above.
Results may differ from the reference program's by a relative error of at most 0.0045.
Values may be sent and summed in bfloat16 or wider, within the bound.
A program may use at most 64 MiB of HBM per device.

```python
import math
import jax
import jax.numpy as jnp
from jax import lax

D_OBS = 512
HID = 1024
ACT = 128
NEWS = 32
POPN = 16
OBS = 2048


def touch_ends(drawn, key, smallest, largest):
    shape = drawn.shape
    place = [jax.random.randint(jax.random.fold_in(key, axis), (), 0, shape[axis]) for axis in range(len(shape))]
    drawn = drawn.at[tuple(place)].set(smallest)
    longest = shape.index(max(shape))
    place[longest] = (place[longest] + 1) % shape[longest]
    return drawn.at[tuple(place)].set(largest)


def block_scale(own_key, extent, split, low, largest):
    def one(axis_at, blocks):
        steps = jax.random.uniform(jax.random.fold_in(jax.random.fold_in(own_key, 6), axis_at), (blocks,), jnp.float32, low / len(split), largest / len(split))
        return jnp.repeat(jnp.exp(steps), extent[axis_at] // blocks).reshape((-1,) + (1,) * (len(extent) - axis_at - 1))

    factor_of = one(*split[0])
    for cut in split[1:]:
        factor_of = factor_of * one(*cut)
    return factor_of


def bell_draw(own_key, dims, deviation, most, pieces=(), kind=jnp.bfloat16):
    level = block_scale(own_key, dims, pieces, -0.22, 0.18) if pieces else 1.0
    result = jax.random.normal(own_key, dims, jnp.float32) * deviation * level
    return jnp.minimum(jnp.maximum(result, -most), most).astype(kind)


def setup_inputs(seed: int = 0) -> dict:
    key_list = jax.random.split(jax.random.key(seed), 8)
    return {
        "observations": bell_draw(key_list[0], (OBS, D_OBS), 1.0, 6.0, ((0, 8),)),
        "rewards": bell_draw(key_list[1], (OBS, ACT), 1.0, 6.0, ((0, 8),)),
        "new_first": bell_draw(key_list[2], (NEWS, D_OBS, HID), D_OBS ** -0.5, 0.25, ((0, 16),)),
        "new_second": bell_draw(key_list[3], (NEWS, HID, D_OBS), HID ** -0.5, 0.1875, ((0, 16),)),
        "pop_first": bell_draw(key_list[4], (POPN, D_OBS, HID), D_OBS ** -0.5, 0.25, ((0, 16),)),
        "pop_second": bell_draw(key_list[5], (POPN, HID, ACT), HID ** -0.5, 0.1875, ((0, 16),)),
        "faces": touch_ends((jax.random.randint(key_list[6], (NEWS, POPN), 0, 4) < 3).astype(jnp.int32), jax.random.fold_in(key_list[6], 1), 0, 1),
    }


def new_states(observations, first, second):
    inner = jax.nn.gelu(jnp.dot(observations, first, preferred_element_type=jnp.float32)).astype(jnp.bfloat16)
    action = jnp.tanh(jnp.dot(inner, second, preferred_element_type=jnp.float32))
    return (observations.astype(jnp.float32) + action).astype(jnp.bfloat16)

def opponent_scores(flat_states, first, second, rewards, groups):
    hidden = jax.nn.gelu(jnp.dot(flat_states, first, preferred_element_type=jnp.float32)).astype(jnp.bfloat16)
    logits = jnp.dot(hidden, second, preferred_element_type=jnp.float32)
    valued = jnp.tanh(logits).reshape(groups, rewards.shape[0], rewards.shape[1]) * rewards.astype(jnp.float32)[None]
    return lax.optimization_barrier(jnp.sum(valued, axis=(1, 2)))

def reference(observations, rewards, new_first, new_second, pop_first, pop_second, faces):
    states = lax.map(lambda pair: new_states(observations, pair[0], pair[1]), (new_first, new_second))
    flat_states = states.reshape(-1, states.shape[2])
    groups = states.shape[0]
    scores = lax.map(lambda pair: opponent_scores(flat_states, pair[0], pair[1], rewards, groups), (pop_first, pop_second))
    scale = 1.0 / math.sqrt(OBS * ACT)
    return jnp.transpose(scores) * scale * faces.astype(jnp.float32)
```

```python
import functools
import math

import jax
import jax.numpy as jnp
from jax import lax
from jax.experimental import pallas as pl
from jax.experimental.pallas import tpu as pltpu
from jax.sharding import PartitionSpec as P

MESH = pl.DeviceIdType.MESH
C0 = math.sqrt(2.0 / math.pi)
C1 = 0.044715 * C0
CFG = dict(compute=True, ysend=True, psend=True, final=True)


def twice_gelu(x):
    return (x + x * jnp.tanh(x * (C0 + C1 * (x * x)))).astype(jnp.bfloat16)


def dot(a, b):
    return jnp.dot(a, b, preferred_element_type=jnp.float32)


def kernel(scale, obs_hbm, rew_hbm, nf_hbm, ns_hbm, pf_hbm, ps_hbm, faces_hbm, out_ref,
           obs, rew, nf, ns, w1, w2, faces, states, part, landed,
           load_sem, ysend_sem, yrecv_sem, psend_sem, precv_sem, out_send, out_recv, hand):
    pop = lax.axis_index("pop")
    batch = lax.axis_index("batch")
    c = lax.rem(pop, 2)
    xl = lax.rem(lax.div(pop, 2), 2)
    y = lax.div(pop, 4)
    h = lax.rem(batch, 2)
    z = lax.div(batch, 2)

    def at(dy=0, dx=0, dc=0, dz=0, dh=0):
        py = lax.rem(y + dy, 4)
        px = lax.rem(xl + dx, 2)
        pc = lax.rem(c + dc, 2)
        return {
            "pop": (py * 2 + px) * 2 + pc,
            "batch": lax.rem(z + dz, 4) * 2 + lax.rem(h + dh, 2),
        }

    left, right, far = at(dy=3), at(dy=1), at(dy=2)
    inner, outer, sibling = at(dx=1), at(dx=1, dh=1), at(dc=1)
    up, down = at(dz=1), at(dz=3)

    loads = [
        pltpu.make_async_copy(src, dst, load_sem.at[i])
        for i, (src, dst) in enumerate([
            (obs_hbm, obs), (nf_hbm.at[0], nf.at[0]), (ns_hbm.at[0], ns.at[0]),
            (nf_hbm.at[1], nf.at[1]), (ns_hbm.at[1], ns.at[1]),
            (pf_hbm.at[0], w1.at[0]), (ps_hbm.at[0], w2.at[0]),
            (rew_hbm, rew), (faces_hbm, faces)])
    ]
    for load in loads:
        load.start()

    barrier = pltpu.get_barrier_semaphore()
    for to in (left, right, inner, outer, sibling, up, down):
        pl.semaphore_signal(barrier, inc=1, device_id=to, device_id_type=MESH)
    pl.semaphore_wait(barrier, 7)

    def greet(level, targets):
        for to in targets:
            pl.semaphore_signal(hand.at[level], inc=1, device_id=to, device_id_type=MESH)

    def greeted(level, count):
        pl.semaphore_wait(hand.at[level], count)

    greet(0, (left, right, inner, outer, up, down))

    def remote(src, dst, ss, rs, to):
        return pltpu.make_async_remote_copy(src_ref=src, dst_ref=dst, send_sem=ss, recv_sem=rs,
                                            device_id=to, device_id_type=MESH)

    pcopies = []

    def psend(src, dst, to):
        k = len(pcopies)
        copy = remote(src, dst, psend_sem.at[k], precv_sem.at[k], to)
        copy.start()
        pcopies.append(copy)
        return copy

    if CFG["psend"]:
        in1 = psend(pf_hbm.at[0, pl.ds(0, 256)], w1.at[2, pl.ds(0, 256)], inner)
        out1 = psend(pf_hbm.at[0, pl.ds(256, 256)], w1.at[2, pl.ds(256, 256)], outer)
        in2 = psend(ps_hbm.at[0, pl.ds(0, 512)], w2.at[2, pl.ds(0, 512)], inner)
        out2 = psend(ps_hbm.at[0, pl.ds(512, 512)], w2.at[2, pl.ds(512, 512)], outer)
        sib1 = psend(pf_hbm.at[0], w1.at[1], sibling)
        sib2 = psend(ps_hbm.at[0], w2.at[1], sibling)

    loads[0].wait()
    ycopies = {}

    def ysend(name, k, slot_from, slot_to, half, to):
        if not CFG["ysend"]:
            return
        rows = pl.ds(half * 128, 128)
        copy = remote(states.at[slot_from, rows], states.at[slot_to, rows],
                      ysend_sem.at[k], yrecv_sem.at[k], to)
        copy.start()
        ycopies[name] = copy

    for a in range(2):
        loads[1 + 2 * a].wait()
        loads[2 + 2 * a].wait()
        if CFG["compute"]:
            inner_h = twice_gelu(dot(obs[...], nf[a]))
            action = jnp.tanh(0.5 * dot(inner_h, ns[a]))
            states[a] = (obs[...].astype(jnp.float32) + action).astype(jnp.bfloat16)
        ysend(("R", a, 0), 0 + 2 * a, a, 2 + 2 * a, 0, right)
        ysend(("L", a, 1), 6 + 2 * a, a, 3 + 2 * a, 1, left)
        ysend(("R", a, 1), 1 + 2 * a, a, 2 + 2 * a, 1, right)
        ysend(("L", a, 0), 7 + 2 * a, a, 3 + 2 * a, 0, left)

    greeted(0, 6)
    greet(1, (left, right, far))
    for i in (5, 6, 7, 8):
        loads[i].wait()

    def score(slot, rel, p):
        if not CFG["compute"]:
            return
        s = states[pl.ds(slot, 2)].reshape(512, 512)
        hidden = twice_gelu(dot(s, w1[p]))
        logits = jnp.tanh(0.5 * dot(hidden, w2[p]))
        k = lax.rem(xl + p // 2, 2) * 2 + lax.rem(c + p % 2, 2)
        r = rew[...].astype(jnp.float32)
        for i in range(2):
            dy, a = rel[i]
            v = jnp.sum(logits[i * 256:(i + 1) * 256] * r, axis=0, keepdims=True)
            part[dy, pl.ds(a * 4 + k, 1), :] = v

    own = ((0, 0), (0, 1))
    g1 = ((3, 0), (1, 0))
    g2 = ((3, 1), (1, 1))
    g3 = ((2, 0), (2, 1))

    def yrecv(*names):
        if CFG["ysend"]:
            for n in names:
                ycopies[n].wait_recv()

    score(0, own, 0)
    if CFG["psend"]:
        sib1.wait_recv()
        sib2.wait_recv()
    score(0, own, 1)
    greeted(1, 3)
    greet(2, (up, down, at(dz=2)))
    yrecv(("R", 0, 0), ("L", 0, 1))
    ysend(("R", 2, 0), 4, 2, 6, 0, right)
    ysend(("L", 2, 1), 10, 3, 6, 1, left)
    yrecv(("R", 0, 1), ("L", 0, 0))
    score(2, g1, 0)
    score(2, g1, 1)
    greeted(2, 3)
    greet(3, (at(dh=1),))
    yrecv(("R", 1, 0), ("L", 1, 1))
    ysend(("R", 3, 0), 5, 4, 7, 0, right)
    ysend(("L", 3, 1), 11, 5, 7, 1, left)
    yrecv(("R", 1, 1), ("L", 1, 0))
    score(4, g2, 0)
    score(4, g2, 1)
    greeted(3, 1)
    if CFG["psend"]:
        for cp in (in1, in2):
            cp.wait_recv()
        r1 = psend(w1.at[2, pl.ds(0, 256)], w1.at[3, pl.ds(0, 256)], sibling)
        r2 = psend(w2.at[2, pl.ds(0, 512)], w2.at[3, pl.ds(0, 512)], sibling)
        for cp in (out1, out2):
            cp.wait_recv()
        r3 = psend(w1.at[2, pl.ds(256, 256)], w1.at[3, pl.ds(256, 256)], sibling)
        r4 = psend(w2.at[2, pl.ds(512, 512)], w2.at[3, pl.ds(512, 512)], sibling)
    for slot, g in ((0, own), (2, g1), (4, g2)):
        score(slot, g, 2)
    if CFG["psend"]:
        for cp in (r1, r2, r3, r4):
            cp.wait_recv()
    for slot, g in ((0, own), (2, g1), (4, g2)):
        score(slot, g, 3)
    yrecv(("R", 2, 0), ("L", 2, 1), ("R", 3, 0), ("L", 3, 1))
    for p in range(4):
        score(6, g3, p)

    me = y * 8 + z * 2 + h
    landed[me] = part[0]
    if CFG["final"]:
        order = sorted(
            [(dy, dz, dh) for dy in range(4) for dz in range(4) for dh in range(2)][1:],
            key=lambda d: -(min(d[0], 4 - d[0]) + min(d[1], 4 - d[1]) + 2 * d[2]))
        for dy, dz, dh in order:
            remote(part.at[dy], landed.at[me], out_send.at[0], out_recv.at[0],
                   at(dy=dy, dz=dz, dh=dh)).start()
        pltpu.make_async_copy(landed.at[pl.ds(0, 31)], landed.at[pl.ds(0, 31)], out_recv.at[0]).wait()
    row = lax.broadcasted_iota(jnp.int32, (8, 16), 0)
    lane = lax.broadcasted_iota(jnp.int32, (8, 16), 1)
    spread = jnp.zeros((8, 16), jnp.float32)
    for ys in range(4):
        total = jnp.sum(landed[pl.ds(ys * 8, 8)], axis=0)
        value = jnp.sum(total, axis=1, keepdims=True)
        spread = spread + jnp.where(lane == ys * 4 + lax.rem(row, 4), value, 0.0)
    gain = faces[...].astype(jnp.float32) * scale
    for a in range(2):
        out_ref[pl.ds(a, 1), :] = jnp.sum(spread[a * 4:(a + 1) * 4], axis=0, keepdims=True) * gain[a:a + 1]

    for copy in list(ycopies.values()) + pcopies:
        copy.wait_send()
    if CFG["final"]:
        pltpu.make_async_copy(landed.at[pl.ds(0, 31)], landed.at[pl.ds(0, 31)], out_send.at[0]).wait()


def body(observations, rewards, new_first, new_second, pop_first, pop_second, faces):
    scale = 1.0 / math.sqrt(observations.shape[0] * lax.axis_size("batch") * rewards.shape[1])
    dma = pltpu.SemaphoreType.DMA
    bf16 = jnp.bfloat16
    return pl.pallas_call(
        functools.partial(kernel, scale),
        out_shape=jax.ShapeDtypeStruct((2, 16), jnp.float32),
        in_specs=[pl.BlockSpec(memory_space=pl.ANY)] * 7,
        out_specs=pl.BlockSpec(memory_space=pltpu.VMEM),
        scratch_shapes=[
            pltpu.VMEM((256, 512), bf16), pltpu.VMEM((256, 128), bf16),
            pltpu.VMEM((2, 512, 1024), bf16), pltpu.VMEM((2, 1024, 512), bf16),
            pltpu.VMEM((4, 512, 1024), bf16), pltpu.VMEM((4, 1024, 128), bf16),
            pltpu.VMEM((2, 16), jnp.int32),
            pltpu.VMEM((8, 256, 512), bf16),
            pltpu.VMEM((4, 8, 128), jnp.float32),
            pltpu.VMEM((32, 8, 128), jnp.float32),
            dma((9,)), dma((12,)), dma((12,)), dma((10,)), dma((10,)), dma((1,)), dma((1,)),
            pltpu.SemaphoreType.REGULAR((4,)),
        ],
        compiler_params=pltpu.CompilerParams(
            collective_id=0, has_side_effects=True, vmem_limit_bytes=60000 * 1024),
    )(observations, rewards, new_first, new_second, pop_first, pop_second, faces)


def solution(mesh):
    placed = (
        P("batch", None),
        P("batch", None),
        P("pop", None, None),
        P("pop", None, None),
        P("pop", None, None),
        P("pop", None, None),
        P("pop", None),
    )
    return jax.shard_map(
        body, mesh=mesh, in_specs=placed, out_specs=P("pop", None), check_vma=False
    )
```

```python
import functools
import math

import jax
import jax.numpy as jnp
from jax import lax
from jax.experimental import pallas as pl
from jax.experimental.pallas import tpu as pltpu
from jax.sharding import PartitionSpec as P

MESH = pl.DeviceIdType.MESH
C0 = math.sqrt(2.0 / math.pi)
C1 = 0.044715 * C0
CFG = dict(compute=True, ysend=True, psend=True, final=True)


def twice_gelu(x):
    return (x + x * jnp.tanh(x * (C0 + C1 * (x * x)))).astype(jnp.bfloat16)


def dot(a, b):
    return jnp.dot(a, b, preferred_element_type=jnp.float32)


PARTS = (
    (0, 128, 0, 0, 0), (128, 128, 0, 0, 128), (256, 128, 0, 1, 0), (384, 128, 0, 1, 128),
    (512, 128, 3, 0, 0), (640, 128, 1, 0, 0), (768, 128, 3, 0, 128), (896, 128, 1, 0, 128),
    (1024, 128, 3, 1, 0), (1152, 128, 1, 1, 128), (1280, 128, 3, 1, 128), (1408, 128, 1, 1, 0),
    (1536, 128, 2, 0, 0), (1664, 128, 2, 0, 128),
    (1792, 64, 2, 1, 0), (1856, 64, 2, 1, 128), (1920, 64, 2, 1, 64), (1984, 64, 2, 1, 192),
)
SENT = {
    "R0": (0, 512, 128), "L0": (0, 640, 128), "R1": (128, 768, 128), "L1": (128, 896, 128),
    "R2": (256, 1024, 128), "L2": (384, 1152, 128), "R3": (384, 1280, 128), "L3": (256, 1408, 128),
    "R4": (512, 1536, 128), "L4": (896, 1664, 128),
    "R5": (1024, 1792, 64), "L5": (1152, 1856, 64), "R6": (1088, 1920, 64), "L6": (1216, 1984, 64),
}


UNITS = ((0, 512), (512, 1024), (512, 768), (768, 1024))


def kernel(scale, obs_hbm, rew_hbm, nf_hbm, ns_hbm, pf_hbm, ps_hbm, faces_hbm, out_ref,
           obs, rew, nf, ns, w1, w2, faces, states, pre, acc, part, message, landed,
           load_sem, ysend_sem, yrecv_sem, psend_sem, precv_sem, out_send, out_recv, hand):
    pop = lax.axis_index("pop")
    batch = lax.axis_index("batch")
    c = lax.rem(pop, 2)
    xl = lax.rem(lax.div(pop, 2), 2)
    y = lax.div(pop, 4)
    h = lax.rem(batch, 2)
    z = lax.div(batch, 2)

    def at(dy=0, dx=0, dc=0, dz=0, dh=0):
        py = lax.rem(y + dy, 4)
        px = lax.rem(xl + dx, 2)
        pc = lax.rem(c + dc, 2)
        return {
            "pop": (py * 2 + px) * 2 + pc,
            "batch": lax.rem(z + dz, 4) * 2 + lax.rem(h + dh, 2),
        }

    left, right, far = at(dy=3), at(dy=1), at(dy=2)
    inner, outer, sibling = at(dx=1), at(dx=1, dh=1), at(dc=1)
    up, down = at(dz=1), at(dz=3)

    barrier = pltpu.get_barrier_semaphore()
    for to in (left, right, inner, outer, sibling, up, down):
        pl.semaphore_signal(barrier, inc=1, device_id=to, device_id_type=MESH)

    loads = [
        pltpu.make_async_copy(src, dst, load_sem.at[i])
        for i, (src, dst) in enumerate([
            (obs_hbm, obs), (nf_hbm.at[0], nf.at[0]), (ns_hbm.at[0], ns.at[0]),
            (nf_hbm.at[1], nf.at[1]), (ns_hbm.at[1], ns.at[1]),
            (pf_hbm.at[0], w1.at[0]), (ps_hbm.at[0], w2.at[0]),
            (rew_hbm, rew), (faces_hbm, faces)])
    ]
    for load in loads:
        load.start()

    def greet(level, targets):
        if not CFG.get("greet",True): return
        for to in targets:
            pl.semaphore_signal(hand.at[level], inc=1, device_id=to, device_id_type=MESH)

    def greeted(level, count):
        if not CFG.get("greet",True): return
        pl.semaphore_wait(hand.at[level], count)

    def remote(src, dst, ss, rs, to):
        return pltpu.make_async_remote_copy(src_ref=src, dst_ref=dst, send_sem=ss, recv_sem=rs,
                                            device_id=to, device_id_type=MESH)

    pcopies = []

    def psend(src, dst, to):
        k = len(pcopies)
        copy = remote(src, dst, psend_sem.at[k], precv_sem.at[k], to)
        copy.start()
        pcopies.append(copy)
        return copy

    ycopies = {}

    def ysend(*names):
        if not CFG["ysend"]:
            return
        for name in names:
            k = len(ycopies)
            here, there, n = SENT[name]
            copy = remote(states.at[pl.ds(here, n)], states.at[pl.ds(there, n)],
                          ysend_sem.at[k], yrecv_sem.at[k], right if name[0] == "R" else left)
            copy.start()
            ycopies[name] = copy

    def yrecv(*names):
        if CFG["ysend"]:
            for n in names:
                ycopies[n].wait_recv()

    def new_states(a, first, n):
        if CFG["compute"]:
            seen = obs[first:first + n]
            inside = twice_gelu(dot(seen, nf[a]))
            action = jnp.tanh(0.5 * dot(inside, ns[a]))
            at_row = a * 256 + first
            states[at_row:at_row + n] = (seen.astype(jnp.float32) + action).astype(jnp.bfloat16)

    part[...] = jnp.zeros_like(part)
    for i in (0, 1, 2):
        loads[i].wait()
    new_states(0, 0, 128)
    pl.semaphore_wait(barrier, 7)
    ysend("R0", "L0")
    xq = []
    sib = []
    if CFG["psend"]:
        sib = [psend(pf_hbm.at[0], w1.at[1], sibling), psend(ps_hbm.at[0], w2.at[1], sibling)]
        for q in range(4):
            cols = pl.ds(q * 256, 256)
            got = []
            for side, to in ((0, inner), (1, outer)):
                rows = pl.ds(side * 256, 256)
                got.append(psend(pf_hbm.at[0, rows, cols], w1.at[2, rows, cols], to))
                if q % 2 == 0:
                    r2 = pl.ds((q + side) * 256, 256)
                    got.append(psend(ps_hbm.at[0, r2], w2.at[2, r2], to))
            xq.append(got)
    new_states(0, 128, 128)
    ysend("R1", "L1")
    for i in (3, 4):
        loads[i].wait()
    new_states(1, 0, 256)
    ysend("R2", "L2", "R3", "L3")
    greet(0, (left, right, inner, outer, up, down))
    for i in (5, 6, 7, 8):
        loads[i].wait()

    relays = []

    def relay(q):
        if not CFG["psend"]:
            return
        for copy in xq[q]:
            copy.wait_recv()
        cols = pl.ds(q * 256, 256)
        got = [psend(w1.at[2, :, cols], w1.at[3, :, cols], sibling)]
        if q % 2 == 0:
            r2 = pl.ds(q * 256, 512)
            got.append(psend(w2.at[2, r2], w2.at[3, r2], sibling))
        relays.append(got)

    def relayed(q):
        if CFG["psend"]:
            for copy in relays[q]:
                copy.wait_recv()

    pending = []
    count = [0]

    def first_layer(first, n, p, half):
        buf = count[0] % 2
        count[0] += 1
        begin, end = UNITS[half]
        pre[buf, :n, :end - begin] = dot(states[first:first + n], w1[p, :, begin:end])
        pending.append((buf, first, n, p, half))

    def second_layer():
        buf, first, n, p, half = pending.pop(0)
        begin, end = UNITS[half]
        d = dot(twice_gelu(pre[buf, :n, :end - begin]), w2[p, begin:end, :])
        if begin == 0:
            acc[p, first:first + n, :] = d
            return
        if end < 1024:
            acc[p, first:first + n, :] += d
            return
        value = jnp.tanh(0.5 * (acc[p, first:first + n, :] + d))
        k = lax.rem(xl + p // 2, 2) * 2 + lax.rem(c + p % 2, 2)
        for row0, rows, dy, a, seen in PARTS:
            if first <= row0 < first + n:
                r = rew[seen:seen + rows].astype(jnp.float32)
                v = jnp.sum(value[row0 - first:row0 - first + rows] * r, axis=0, keepdims=True)
                part[dy, pl.ds(a * 4 + k, 1), :] += v

    def run(pieces, flush=True):
        if not CFG["compute"]:
            return
        for piece in pieces:
            first_layer(*piece)
            if len(pending) > 1:
                second_layer()
        if flush and pending:
            second_layer()

    def whole(first, n, *ps):
        return [(first, n, p, half) for p in ps for half in (0, 1)]

    for copy in sib:
        copy.wait_recv()
    run(whole(0, 512, 0, 1))
    yrecv("R0", "L0")
    ysend("R4")
    run(whole(512, 256, 0, 1))
    relay(0)
    greeted(0, 6)
    greet(1, (left, right, far))
    yrecv("R1", "L1")
    ysend("L4")
    run(whole(768, 256, 0, 1), flush=False)
    relay(1)
    run([(0, 512, 2, 0), (512, 512, 2, 0)])
    greeted(1, 3)
    greet(2, (up, down, at(dz=2)))
    yrecv("R2", "L2")
    ysend("R5", "L5", "R6", "L6")
    run(whole(1024, 256, 0, 1), flush=False)
    relayed(0)
    relayed(1)
    run([(0, 512, 3, 0), (512, 512, 3, 0)])
    yrecv("R3", "L3")
    relay(2)
    run(whole(1280, 256, 0, 1) + [(1024, 512, 2, 0), (1024, 512, 3, 0)]
        + [(first, 512, 2, 2) for first in (0, 512, 1024)], flush=False)
    relayed(2)
    greeted(2, 3)
    greet(3, (at(dh=1),))
    run([(first, 512, 3, 2) for first in (0, 512, 1024)], flush=False)
    yrecv("R4", "L4")
    run(whole(1536, 256, 0, 1))
    relay(3)
    run([(first, 512, 2, 3) for first in (0, 512, 1024)] + whole(1536, 256, 2), flush=False)
    relayed(3)
    run([(first, 512, 3, 3) for first in (0, 512, 1024)] + whole(1536, 256, 3), flush=False)
    yrecv("R5", "L5")
    run(whole(1792, 128, 0, 1, 2, 3))
    greeted(3, 1)

    row = lax.broadcasted_iota(jnp.int32, (8, 128), 0)
    lane = lax.broadcasted_iota(jnp.int32, (8, 128), 1)
    place = lane == lax.div(row, 4) * 16 + y * 4 + lax.rem(row, 4)
    me = y * 8 + z * 2 + h

    def deliver(*dys):
        for dy in dys:
            value = jnp.sum(part[dy], axis=1, keepdims=True)
            message[dy] = jnp.sum(jnp.where(place, value, 0.0), axis=0, keepdims=True)
        if 0 in dys:
            landed[me] = message[0]
        if CFG["final"]:
            order = sorted(
                [(dy, dz, dh) for dy in dys for dz in range(4) for dh in range(2)
                 if (dy, dz, dh) != (0, 0, 0)],
                key=lambda d: -(min(d[0], 4 - d[0]) + min(d[1], 4 - d[1]) + 2 * d[2]))
            for dy, dz, dh in order:
                remote(message.at[dy], landed.at[me], out_send.at[0], out_recv.at[0],
                       at(dy=dy, dz=dz, dh=dh)).start()

    deliver(0, 1, 3)
    yrecv("R6", "L6")
    run(whole(1920, 128, 0, 1, 2, 3))
    deliver(2)
    if CFG["final"]:
        pltpu.make_async_copy(landed.at[pl.ds(0, 31)], landed.at[pl.ds(0, 31)], out_recv.at[0]).wait()
    total = jnp.sum(landed[...].reshape(32, 128), axis=0, keepdims=True)
    gain = faces[...].astype(jnp.float32) * scale
    for a in range(2):
        out_ref[pl.ds(a, 1), :] = total[:, a * 16:(a + 1) * 16] * gain[a:a + 1]

    for copy in list(ycopies.values()) + pcopies:
        copy.wait_send()
    if CFG["final"]:
        pltpu.make_async_copy(landed.at[pl.ds(0, 31)], landed.at[pl.ds(0, 31)], out_send.at[0]).wait()


def body(observations, rewards, new_first, new_second, pop_first, pop_second, faces):
    scale = 1.0 / math.sqrt(observations.shape[0] * lax.axis_size("batch") * rewards.shape[1])
    dma = pltpu.SemaphoreType.DMA
    bf16 = jnp.bfloat16
    return pl.pallas_call(
        functools.partial(kernel, scale),
        out_shape=jax.ShapeDtypeStruct((2, 16), jnp.float32),
        in_specs=[pl.BlockSpec(memory_space=pl.ANY)] * 7,
        out_specs=pl.BlockSpec(memory_space=pltpu.VMEM),
        scratch_shapes=[
            pltpu.VMEM((256, 512), bf16), pltpu.VMEM((256, 128), bf16),
            pltpu.VMEM((2, 512, 1024), bf16), pltpu.VMEM((2, 1024, 512), bf16),
            pltpu.VMEM((4, 512, 1024), bf16), pltpu.VMEM((4, 1024, 128), bf16),
            pltpu.VMEM((2, 16), jnp.int32),
            pltpu.VMEM((2048, 512), bf16),
            pltpu.VMEM((2, 512, 512), jnp.float32),
            pltpu.VMEM((4, 2048, 128), jnp.float32),
            pltpu.VMEM((4, 8, 128), jnp.float32),
            pltpu.VMEM((4, 1, 128), jnp.float32),
            pltpu.VMEM((32, 1, 128), jnp.float32),
            dma((9,)), dma((14,)), dma((14,)), dma((20,)), dma((20,)), dma((1,)), dma((1,)),
            pltpu.SemaphoreType.REGULAR((4,)),
        ],
        compiler_params=pltpu.CompilerParams(
            collective_id=0, has_side_effects=True, vmem_limit_bytes=60000 * 1024),
    )(observations, rewards, new_first, new_second, pop_first, pop_second, faces)


def solution(mesh):
    placed = (
        P("batch", None),
        P("batch", None),
        P("pop", None, None),
        P("pop", None, None),
        P("pop", None, None),
        P("pop", None, None),
        P("pop", None),
    )
    return jax.shard_map(
        body, mesh=mesh, in_specs=placed, out_specs=P("pop", None), check_vma=False
    )
```

```python
import functools
import math

import jax
import jax.numpy as jnp
from jax import lax
from jax.experimental import pallas as pl
from jax.experimental.pallas import tpu as pltpu
from jax.sharding import PartitionSpec as P

MESH = pl.DeviceIdType.MESH
C0 = math.sqrt(2.0 / math.pi)
C1 = 0.044715 * C0
CFG = dict(compute=True, ysend=True, psend=True, final=True)


def twice_gelu(x):
    return (x + x * jnp.tanh(x * (C0 + C1 * (x * x)))).astype(jnp.bfloat16)


def dot(a, b):
    return jnp.dot(a, b, preferred_element_type=jnp.float32)


PARTS = (
    (0, 128, 0, 0, 0), (128, 128, 0, 0, 128), (256, 128, 0, 1, 0), (384, 128, 0, 1, 128),
    (512, 128, 3, 0, 0), (640, 128, 1, 0, 0), (768, 128, 3, 0, 128), (896, 128, 1, 0, 128),
    (1024, 128, 3, 1, 0), (1152, 128, 1, 1, 128), (1280, 128, 3, 1, 128), (1408, 128, 1, 1, 0),
    (1536, 128, 2, 0, 0), (1664, 128, 2, 0, 128),
    (1792, 64, 2, 1, 0), (1856, 64, 2, 1, 128), (1920, 64, 2, 1, 64), (1984, 64, 2, 1, 192),
)
SENT = {
    "R0": (0, 512, 128), "L0": (0, 640, 128), "R1": (128, 768, 128), "L1": (128, 896, 128),
    "R2": (256, 1024, 128), "L2": (384, 1152, 128), "R3": (384, 1280, 128), "L3": (256, 1408, 128),
    "R4": (512, 1536, 128), "L4": (896, 1664, 128),
    "R5": (1024, 1792, 64), "L5": (1152, 1856, 64), "R6": (1088, 1920, 64), "L6": (1216, 1984, 64),
}


UNITS = ((0, 512), (512, 1024), (512, 768), (768, 1024))


def kernel(scale, obs_hbm, rew_hbm, nf_hbm, ns_hbm, pf_hbm, ps_hbm, faces_hbm, out_ref,
           obs, rew, nf, ns, w1, w2, faces, states, pre, acc, part, message, landed,
           load_sem, ysend_sem, yrecv_sem, psend_sem, precv_sem, out_send, out_recv, hand):
    pop = lax.axis_index("pop")
    batch = lax.axis_index("batch")
    c = lax.rem(pop, 2)
    xl = lax.rem(lax.div(pop, 2), 2)
    y = lax.div(pop, 4)
    h = lax.rem(batch, 2)
    z = lax.div(batch, 2)

    def at(dy=0, dx=0, dc=0, dz=0, dh=0):
        py = lax.rem(y + dy, 4)
        px = lax.rem(xl + dx, 2)
        pc = lax.rem(c + dc, 2)
        return {
            "pop": (py * 2 + px) * 2 + pc,
            "batch": lax.rem(z + dz, 4) * 2 + lax.rem(h + dh, 2),
        }

    left, right, far = at(dy=3), at(dy=1), at(dy=2)
    inner, outer, sibling = at(dx=1), at(dx=1, dh=1), at(dc=1)
    up, down = at(dz=1), at(dz=3)

    barrier = pltpu.get_barrier_semaphore()
    for to in (left, right, inner, outer, sibling, up, down):
        pl.semaphore_signal(barrier, inc=1, device_id=to, device_id_type=MESH)

    loads = [
        pltpu.make_async_copy(src, dst, load_sem.at[i])
        for i, (src, dst) in enumerate([
            (obs_hbm, obs), (nf_hbm.at[0], nf.at[0]), (ns_hbm.at[0], ns.at[0]),
            (nf_hbm.at[1], nf.at[1]), (ns_hbm.at[1], ns.at[1]),
            (pf_hbm.at[0], w1.at[0]), (ps_hbm.at[0], w2.at[0]),
            (rew_hbm, rew), (faces_hbm, faces)])
    ]
    for load in loads:
        load.start()

    def greet(level, targets):
        if not CFG.get("greet",True): return
        for to in targets:
            pl.semaphore_signal(hand.at[level], inc=1, device_id=to, device_id_type=MESH)

    def greeted(level, count):
        if not CFG.get("greet",True): return
        pl.semaphore_wait(hand.at[level], count)

    def remote(src, dst, ss, rs, to):
        return pltpu.make_async_remote_copy(src_ref=src, dst_ref=dst, send_sem=ss, recv_sem=rs,
                                            device_id=to, device_id_type=MESH)

    pcopies = []

    def psend(src, dst, to):
        k = len(pcopies)
        copy = remote(src, dst, psend_sem.at[k], precv_sem.at[k], to)
        copy.start()
        pcopies.append(copy)
        return copy

    ycopies = {}

    def ysend(*names):
        if not CFG["ysend"]:
            return
        for name in names:
            k = len(ycopies)
            here, there, n = SENT[name]
            copy = remote(states.at[pl.ds(here, n)], states.at[pl.ds(there, n)],
                          ysend_sem.at[k], yrecv_sem.at[k], right if name[0] == "R" else left)
            copy.start()
            ycopies[name] = copy

    def yrecv(*names):
        if CFG["ysend"]:
            for n in names:
                ycopies[n].wait_recv()

    def new_states(a, first, n):
        if CFG["compute"]:
            seen = obs[first:first + n]
            inside = twice_gelu(dot(seen, nf[a]))
            action = jnp.tanh(0.5 * dot(inside, ns[a]))
            at_row = a * 256 + first
            states[at_row:at_row + n] = (seen.astype(jnp.float32) + action).astype(jnp.bfloat16)

    part[...] = jnp.zeros_like(part)
    for i in (0, 1, 2):
        loads[i].wait()
    new_states(0, 0, 128)
    pl.semaphore_wait(barrier, 7)
    ysend("R0", "L0")
    xq = []
    sib = []
    if CFG["psend"]:
        sib = [psend(pf_hbm.at[0], w1.at[1], sibling), psend(ps_hbm.at[0], w2.at[1], sibling)]
        for q in range(4):
            cols = pl.ds(q * 256, 256)
            got = []
            for side, to in ((0, inner), (1, outer)):
                rows = pl.ds(side * 256, 256)
                got.append(psend(pf_hbm.at[0, rows, cols], w1.at[2, rows, cols], to))
                if q % 2 == 0:
                    r2 = pl.ds((q + side) * 256, 256)
                    got.append(psend(ps_hbm.at[0, r2], w2.at[2, r2], to))
            xq.append(got)
    new_states(0, 128, 128)
    ysend("R1", "L1")
    for i in (3, 4):
        loads[i].wait()
    new_states(1, 0, 256)
    ysend("R2", "L2", "R3", "L3")
    greet(0, (left, right, inner, outer, up, down))
    for i in (5, 6, 7, 8):
        loads[i].wait()

    relays = []

    def relay(q):
        if not CFG["psend"]:
            return
        for copy in xq[q]:
            copy.wait_recv()
        cols = pl.ds(q * 256, 256)
        got = [psend(w1.at[2, :, cols], w1.at[3, :, cols], sibling)]
        if q % 2 == 0:
            r2 = pl.ds(q * 256, 512)
            got.append(psend(w2.at[2, r2], w2.at[3, r2], sibling))
        relays.append(got)

    def relayed(q):
        if CFG["psend"]:
            for copy in relays[q]:
                copy.wait_recv()

    pending = []
    count = [0]

    def first_layer(first, n, p, half):
        buf = count[0] % 2
        count[0] += 1
        begin, end = UNITS[half]
        pre[buf, :n, :end - begin] = dot(states[first:first + n], w1[p, :, begin:end])
        pending.append((buf, first, n, p, half))

    def second_layer():
        buf, first, n, p, half = pending.pop(0)
        begin, end = UNITS[half]
        d = dot(twice_gelu(pre[buf, :n, :end - begin]), w2[p, begin:end, :])
        if begin == 0:
            acc[p, first:first + n, :] = d
            return
        if end < 1024:
            acc[p, first:first + n, :] += d
            return
        value = jnp.tanh(0.5 * (acc[p, first:first + n, :] + d))
        k = lax.rem(xl + p // 2, 2) * 2 + lax.rem(c + p % 2, 2)
        for row0, rows, dy, a, seen in PARTS:
            if first <= row0 < first + n:
                r = rew[seen:seen + rows].astype(jnp.float32)
                v = jnp.sum(value[row0 - first:row0 - first + rows] * r, axis=0, keepdims=True)
                part[dy, pl.ds(a * 4 + k, 1), :] += v

    def run(pieces, flush=True):
        if not CFG["compute"]:
            return
        for piece in pieces:
            first_layer(*piece)
            if len(pending) > 1:
                second_layer()
        if flush and pending:
            second_layer()

    def whole(first, n, *ps):
        return [(first, n, p, half) for p in ps for half in (0, 1)]

    for copy in sib:
        copy.wait_recv()
    run(whole(0, 512, 0, 1))
    yrecv("R0", "L0")
    ysend("R4")
    run(whole(512, 256, 0, 1))
    relay(0)
    greeted(0, 6)
    greet(1, (left, right, far))
    yrecv("R1", "L1")
    ysend("L4")
    run(whole(768, 256, 0, 1), flush=False)
    relay(1)
    run([(0, 512, 2, 0), (512, 512, 2, 0)])
    greeted(1, 3)
    greet(2, (up, down, at(dz=2)))
    yrecv("R2", "L2")
    ysend("R5", "L5", "R6", "L6")
    run(whole(1024, 256, 0, 1), flush=False)
    relayed(0)
    relayed(1)
    run([(0, 512, 3, 0), (512, 512, 3, 0)])
    yrecv("R3", "L3")
    relay(2)
    run(whole(1280, 256, 0, 1) + [(1024, 512, 2, 0), (1024, 512, 3, 0)]
        + [(first, 512, 2, 2) for first in (0, 512, 1024)], flush=False)
    relayed(2)
    greeted(2, 3)
    greet(3, (at(dh=1),))
    run([(first, 512, 3, 2) for first in (0, 512, 1024)], flush=False)
    yrecv("R4", "L4")
    run(whole(1536, 256, 0, 1))
    relay(3)
    run([(first, 512, 2, 3) for first in (0, 512, 1024)] + whole(1536, 256, 2), flush=False)
    relayed(3)
    run([(first, 512, 3, 3) for first in (0, 512, 1024)] + whole(1536, 256, 3))
    greeted(3, 1)

    row = lax.broadcasted_iota(jnp.int32, (8, 128), 0)
    lane = lax.broadcasted_iota(jnp.int32, (8, 128), 1)
    place = lane == lax.div(row, 4) * 16 + y * 4 + lax.rem(row, 4)
    me = y * 8 + z * 2 + h

    def deliver(*dys):
        for dy in dys:
            value = jnp.sum(part[dy], axis=1, keepdims=True)
            message[dy] = jnp.sum(jnp.where(place, value, 0.0), axis=0, keepdims=True)
        if 0 in dys:
            landed[me] = message[0]
        if CFG["final"]:
            order = sorted(
                [(dy, dz, dh) for dy in dys for dz in range(4) for dh in range(2)
                 if (dy, dz, dh) != (0, 0, 0)],
                key=lambda d: -(min(d[0], 4 - d[0]) + min(d[1], 4 - d[1]) + 2 * d[2]))
            for dy, dz, dh in order:
                remote(message.at[dy], landed.at[me], out_send.at[0], out_recv.at[0],
                       at(dy=dy, dz=dz, dh=dh)).start()

    deliver(0, 1, 3)
    yrecv("R5", "L5", "R6", "L6")
    run(whole(1792, 256, 0, 1, 2, 3))
    deliver(2)
    if CFG["final"]:
        pltpu.make_async_copy(landed.at[pl.ds(0, 31)], landed.at[pl.ds(0, 31)], out_recv.at[0]).wait()
    total = jnp.sum(landed[...].reshape(32, 128), axis=0, keepdims=True)
    gain = faces[...].astype(jnp.float32) * scale
    for a in range(2):
        out_ref[pl.ds(a, 1), :] = total[:, a * 16:(a + 1) * 16] * gain[a:a + 1]

    for copy in list(ycopies.values()) + pcopies:
        copy.wait_send()
    if CFG["final"]:
        pltpu.make_async_copy(landed.at[pl.ds(0, 31)], landed.at[pl.ds(0, 31)], out_send.at[0]).wait()


def body(observations, rewards, new_first, new_second, pop_first, pop_second, faces):
    scale = 1.0 / math.sqrt(observations.shape[0] * lax.axis_size("batch") * rewards.shape[1])
    dma = pltpu.SemaphoreType.DMA
    bf16 = jnp.bfloat16
    return pl.pallas_call(
        functools.partial(kernel, scale),
        out_shape=jax.ShapeDtypeStruct((2, 16), jnp.float32),
        in_specs=[pl.BlockSpec(memory_space=pl.ANY)] * 7,
        out_specs=pl.BlockSpec(memory_space=pltpu.VMEM),
        scratch_shapes=[
            pltpu.VMEM((256, 512), bf16), pltpu.VMEM((256, 128), bf16),
            pltpu.VMEM((2, 512, 1024), bf16), pltpu.VMEM((2, 1024, 512), bf16),
            pltpu.VMEM((4, 512, 1024), bf16), pltpu.VMEM((4, 1024, 128), bf16),
            pltpu.VMEM((2, 16), jnp.int32),
            pltpu.VMEM((2048, 512), bf16),
            pltpu.VMEM((2, 512, 512), jnp.float32),
            pltpu.VMEM((4, 2048, 128), jnp.float32),
            pltpu.VMEM((4, 8, 128), jnp.float32),
            pltpu.VMEM((4, 1, 128), jnp.float32),
            pltpu.VMEM((32, 1, 128), jnp.float32),
            dma((9,)), dma((14,)), dma((14,)), dma((20,)), dma((20,)), dma((1,)), dma((1,)),
            pltpu.SemaphoreType.REGULAR((4,)),
        ],
        compiler_params=pltpu.CompilerParams(
            collective_id=0, has_side_effects=True, vmem_limit_bytes=60000 * 1024),
    )(observations, rewards, new_first, new_second, pop_first, pop_second, faces)


def solution(mesh):
    placed = (
        P("batch", None),
        P("batch", None),
        P("pop", None, None),
        P("pop", None, None),
        P("pop", None, None),
        P("pop", None, None),
        P("pop", None),
    )
    return jax.shard_map(
        body, mesh=mesh, in_specs=placed, out_specs=P("pop", None), check_vma=False
    )
```
